256 devices in a mesh: ka: 16 (over y_lo, z), br: 4 (over y_hi, core), bc: 4 (over x).
Axes of the slice: x: 4, y: 4 (y_hi: 2, y_lo: 2; y = y_hi * 2 + y_lo), z: 8, core: 2. Of those that a mesh axis runs over, the one named last changes fastest.
Arguments:
- green_lesser: float32 [16, 15, 2, 512, 512], P('ka', None, None, 'br', 'bc'), may hold values from -6 to 6
- screened: float32 [5, 8, 2, 512, 512], P(None, None, None, 'br', 'bc'), may hold values from -0.6 to 0.6
- slot_table: int32 [5, 16, 1], P(None, 'ka'), may hold values from 0 to 4
Outputs:
- sigma_lesser: float32 [16, 8, 2, 512, 512], P('ka', None, None, 'br', 'bc')
The draws below stay inside these ranges and needn't reach their ends.
All inputs are finite; a program needn't handle non-finite values.
Results may differ from the reference program's by a relative error of at most 0.0003.
Values sent between devices are 32-bit elements; how exact they have to be, the bound alone decides.
A program may use at most 64 MiB of HBM per device.

```python
import jax
import jax.numpy as jnp
from jax import lax

NA = 512
KD = 1
NE = 8
NW = 8
NQW = 5
STOPS = 5
NK = 16
NEG = 15


def set_ends(drawn, own_key, smallest, high):
    place = [jax.random.randint(jax.random.fold_in(own_key, axis), (), 0, length) for axis, length in enumerate(drawn.shape)]
    longest = drawn.shape.index(max(drawn.shape))
    beside = place[:longest] + [(place[longest] + 1) % drawn.shape[longest]] + place[longest + 1:]
    return drawn.at[tuple(place)].set(smallest).at[tuple(beside)].set(high)


def level_of(key, dims, split, smallest, top_value):
    level = 1.0
    for axis_at, blocks in split:
        draws = jax.random.uniform(jax.random.fold_in(jax.random.fold_in(key, 6), axis_at), (blocks,), jnp.float32, smallest / len(split), top_value / len(split))
        level = level * jnp.repeat(jnp.exp(draws), dims[axis_at] // blocks).reshape((-1,) + (1,) * (len(dims) - 1 - axis_at))
    return level


def gaussian(stream_key, shape, spread, bound, shards=(), kind=jnp.bfloat16):
    gain = level_of(stream_key, shape, shards, -0.22, 0.18) if shards else 1.0
    array = jax.random.normal(stream_key, shape, jnp.float32) * spread * gain
    return jnp.minimum(jnp.maximum(array, -bound), bound).astype(kind)


def setup_inputs(seed: int = 0) -> dict:
    key_list = jax.random.split(jax.random.key(seed), 4)
    return {
        "green_lesser": gaussian(key_list[0], (NK, NEG, 2, NA, NA), 1.0, 6.0, ((0, 16), (3, 4), (4, 4)), jnp.float32),
        "screened": gaussian(key_list[1], (NQW, NW, 2, NA, NA), 0.1, 0.6, ((3, 4), (4, 4)), jnp.float32),
        "slot_table": set_ends(jax.random.randint(key_list[2], (STOPS, NK, KD), 0, NQW), jax.random.fold_in(key_list[2], 1), 0, NQW - 1).astype(jnp.int32),
    }


hop_shifts = (0, 1, -1, 2, -2)


def skew_part(values, transposed):
    return jnp.stack(((values[:, :, 0] - transposed[:, :, 0]) * 0.5, (values[:, :, 1] + transposed[:, :, 1]) * 0.5), 2)


def reference(green_lesser, screened, slot_table):
    def one_momentum(momentum):
        block_start = momentum - momentum % KD
        real_sum = jnp.zeros((NE, NA, NA), jnp.float32)
        imag_sum = jnp.zeros((NE, NA, NA), jnp.float32)
        for stop_index in range(len(hop_shifts)):
            for remote_index in range(KD):
                partner = ((block_start - KD * hop_shifts[stop_index] + remote_index) % NK).astype(jnp.int32)
                remote = lax.dynamic_index_in_dim(green_lesser, partner, 0, keepdims=False)
                slot_index = slot_table[stop_index, momentum, remote_index].astype(jnp.int32)
                chosen = lax.dynamic_index_in_dim(screened, slot_index, 0, keepdims=False)
                for freq_index in range(NW):
                    lag_start = NW - 1 - freq_index
                    window = remote[lag_start:lag_start + NE]
                    green_real = window[:, 0]
                    green_imag = window[:, 1]
                    inter_real = chosen[freq_index, 0]
                    inter_imag = chosen[freq_index, 1]
                    real_sum = real_sum - (green_real * inter_imag + green_imag * inter_real)
                    imag_sum = imag_sum + (green_real * inter_real - green_imag * inter_imag)
        return jnp.stack((real_sum, imag_sum), 1)

    unsymmetric = lax.map(one_momentum, jnp.arange(NK, dtype=jnp.int32))
    transposed = jnp.swapaxes(unsymmetric, -1, -2)
    return skew_part(unsymmetric, transposed)
```

```python
import functools

import jax
import jax.numpy as jnp
from jax import lax
from jax.experimental import pallas as pl
from jax.experimental.pallas import tpu as pltpu
from jax.sharding import PartitionSpec as P

NE = 8
NW = 8
GROUP = 2
MESH = pl.DeviceIdType.MESH
FAR_UP, FAR_DOWN, NEAR_UP, NEAR_DOWN = range(4)
HOPS = (2, -2, 1, -1)
STOPS = (3, 4, 1, 2)
STEPS = (1, -1, 1, -1)


def kernel(
    sizes, green_hbm, screened_hbm, table, out_hbm,
    green, screened, tables, src, rcv, give, take, total, mirror, result, work,
    load_sem, table_send, table_recv, ring_send, ring_recv, pair_send, pair_recv,
    mirror_send, mirror_recv, out_sem,
):
    n_ka = sizes["ka"]
    k, r, c = lax.axis_index("ka"), lax.axis_index("br"), lax.axis_index("bc")
    is_diag = r == c
    is_near = (r // GROUP == c // GROUP) & (r != c)
    is_far = r // GROUP != c // GROUP
    partner = (k, c, r)

    def at_hop(hop):
        return (lax.rem(k + hop + n_ka, n_ka), r, c)

    barrier = pltpu.get_barrier_semaphore()
    for hop in HOPS:
        pl.semaphore_signal(barrier, inc=1, device_id=at_hop(hop), device_id_type=MESH)

    @pl.when(jnp.logical_not(is_diag))
    def _():
        pl.semaphore_signal(barrier, inc=1, device_id=partner, device_id_type=MESH)

    loads = [
        pltpu.make_async_copy(green_hbm.at[0], green, load_sem.at[0]),
        pltpu.make_async_copy(screened_hbm, screened, load_sem.at[1]),
    ]
    for load in loads:
        load.start()

    @pl.when(is_diag)
    def _():
        pl.semaphore_wait(barrier, len(HOPS))

    @pl.when(jnp.logical_not(is_diag))
    def _():
        pl.semaphore_wait(barrier, len(HOPS) + 1)

    def table_copy(i):
        return pltpu.make_async_remote_copy(
            src_ref=table, dst_ref=tables.at[i], send_sem=table_send.at[i], recv_sem=table_recv.at[i],
            device_id=at_hop(-HOPS[i]), device_id_type=MESH,
        )

    for i in range(4):
        table_copy(i).start()
    for load in loads:
        load.wait()
    for i in range(4):
        table_copy(i).wait_recv()
    slots = [tables[i, STOPS[i], 0] for i in range(4)]
    own_slot = table[0, 0]

    def ring_copy(d, j):
        return pltpu.make_async_remote_copy(
            src_ref=src.at[d, j], dst_ref=rcv.at[d, j], send_sem=ring_send.at[d, j], recv_sem=ring_recv.at[d, j],
            device_id=at_hop(STEPS[d]), device_id_type=MESH,
        )

    def pair_copy(d, j):
        return pltpu.make_async_remote_copy(
            src_ref=give.at[d, j], dst_ref=take.at[d, j], send_sem=pair_send.at[d, j], recv_sem=pair_recv.at[d, j],
            device_id=partner, device_id_type=MESH,
        )

    def mirror_copy(e):
        return pltpu.make_async_remote_copy(
            src_ref=total.at[e], dst_ref=mirror.at[e], send_sem=mirror_send.at[e], recv_sem=mirror_recv.at[e],
            device_id=partner, device_id_type=MESH,
        )

    def out_copy(e):
        return pltpu.make_async_copy(result.at[e], out_hbm.at[0, e], out_sem.at[e])

    tile_rows = green.shape[2]

    def terms(dsts, slot, first, added=None):
        count = len(dsts)

        def block(i, carry):
            rows = pl.ds(pl.multiple_of(i * 8, 8), 8)
            real, imag = [None] * count, [None] * count
            window = [[green[first + lag, part, rows, :] for part in range(2)] for lag in range(count + NW - 1)]
            for w in range(NW):
                wr, wi = screened[slot, w, 0, rows, :], screened[slot, w, 1, rows, :]
                for n in range(count):
                    gr, gi = window[n + NW - 1 - w]
                    plus, minus = gr * wi + gi * wr, gr * wr - gi * wi
                    real[n] = -plus if w == 0 else real[n] - plus
                    imag[n] = minus if w == 0 else imag[n] + minus
            for n in range(count):
                if added is not None:
                    real[n] = real[n] + added[0, rows, :]
                    imag[n] = imag[n] + added[1, rows, :]
                dsts[n][0, rows, :] = real[n]
                dsts[n][1, rows, :] = imag[n]
            return carry

        lax.fori_loop(0, tile_rows // 8, block, 0)

    def write_out(e, other):
        result[e, 0] = (total[e, 0] - other[e, 0].T) * 0.5
        result[e, 1] = (total[e, 1] + other[e, 1].T) * 0.5
        out_copy(e).start()

    def each(count, body):
        def step(i, carry):
            body(i)
            return carry

        lax.fori_loop(0, count, step, 0)

    def own_terms(i):
        terms([total.at[2 * i], total.at[2 * i + 1]], own_slot, 2 * i)

    @pl.when(is_far)
    def _():
        def step(i):
            @pl.when(i < NE)
            def _():
                for d in (FAR_UP, FAR_DOWN):
                    terms([src.at[d, i]], slots[d], i)
                    ring_copy(d, i).start()

            @pl.when((i >= 2) & (i < NE + 2))
            def _():
                for d in (NEAR_UP, NEAR_DOWN):
                    ring_copy(d - 2, i - 2).wait_recv()
                    terms([src.at[d, i - 2]], slots[d], i - 2, rcv.at[d - 2, i - 2])
                    ring_copy(d, i - 2).start()

            @pl.when(i < NE)
            def _():
                terms([total.at[i]], own_slot, i)

            @pl.when((i >= 4) & (i < NE + 4))
            def _():
                e = i - 4
                for d in (NEAR_UP, NEAR_DOWN):
                    ring_copy(d, e).wait_recv()
                total[e] = total[e] + (rcv[NEAR_UP, e] + rcv[NEAR_DOWN, e])
                mirror_copy(e).start()

            @pl.when(i >= 5)
            def _():
                e = i - 5
                mirror_copy(e).wait_recv()
                write_out(e, mirror)

        each(NE + 5, step)

        def close(e):
            for d in range(4):
                ring_copy(d, e).wait_send()
            mirror_copy(e).wait_send()

        each(NE, close)

    half = NE // 2

    @pl.when(is_near)
    def _():
        mine = jnp.where(r < c, 0, half)
        theirs = half - mine

        def offer(i):
            for d in range(4):
                terms([give.at[d, i]], slots[d], theirs + i)
                pair_copy(d, i).start()

        def joined(d, j, added):
            terms([work.at[0]], slots[d], mine + j, added)
            pair_copy(d, j).wait_recv()
            src[d, j, 0] = work[0, 0] - take[d, j, 0].T
            src[d, j, 1] = work[0, 1] + take[d, j, 1].T
            ring_copy(d, j).start()

        def step(i):
            @pl.when(i < half)
            def _():
                offer(i)

            @pl.when((i >= 1) & (i < half + 1))
            def _():
                for d in (FAR_UP, FAR_DOWN):
                    joined(d, i - 1, None)

            @pl.when(i < half)
            def _():
                own_terms(i)

            @pl.when((i >= 2) & (i < half + 2))
            def _():
                for d in (NEAR_UP, NEAR_DOWN):
                    ring_copy(d - 2, i - 2).wait_recv()
                    joined(d, i - 2, rcv.at[d - 2, i - 2])

            @pl.when(i == half)
            def _():
                each(half, lambda j: mirror_copy(theirs + j).start())

            @pl.when(i >= 3)
            def _():
                j = i - 3
                e = mine + j
                for d in (NEAR_UP, NEAR_DOWN):
                    ring_copy(d, j).wait_recv()
                total[e] = total[e] + (rcv[NEAR_UP, j] + rcv[NEAR_DOWN, j])

            @pl.when(i == half)
            def _():
                for j in range(2):
                    mirror_copy(mine + j).start()

            @pl.when(i > half)
            def _():
                mirror_copy(mine + i - 3).start()

        each(half + 3, step)

        def finish(j):
            for first in (mine, theirs):
                mirror_copy(first + j).wait_recv()
                write_out(first + j, mirror)

        each(half, finish)

        def close(j):
            for d in range(4):
                ring_copy(d, j).wait_send()
                pair_copy(d, j).wait_send()
            mirror_copy(j).wait_send()
            mirror_copy(half + j).wait_send()

        each(half, close)

    @pl.when(is_diag)
    def _():
        row = lax.broadcasted_iota(jnp.int32, (tile_rows, tile_rows), 0)
        col = lax.broadcasted_iota(jnp.int32, (tile_rows, tile_rows), 1)

        def folded(d, j, added):
            terms([work.at[0], work.at[1]], slots[d], 2 * j)
            real = [work[n, 0] - work[n, 0].T for n in range(2)]
            imag = [work[n, 1] + work[n, 1].T for n in range(2)]
            packed_real = jnp.where(row < col, real[0], jnp.where(row > col, real[1], imag[1]))
            packed_imag = jnp.where(row <= col, imag[0], imag[1])
            if added is not None:
                packed_real, packed_imag = packed_real + added[0], packed_imag + added[1]
            src[d, j, 0] = packed_real
            src[d, j, 1] = packed_imag
            ring_copy(d, j).start()

        def step(i):
            @pl.when(i < half)
            def _():
                for d in (FAR_UP, FAR_DOWN):
                    folded(d, i, None)

            @pl.when((i >= 1) & (i < half + 1))
            def _():
                for d in (NEAR_UP, NEAR_DOWN):
                    ring_copy(d - 2, i - 1).wait_recv()
                    folded(d, i - 1, rcv.at[d - 2, i - 1])

            @pl.when(i < half)
            def _():
                own_terms(i)

            @pl.when(i >= 2)
            def _():
                j = i - 2
                for d in (NEAR_UP, NEAR_DOWN):
                    ring_copy(d, j).wait_recv()
                real = rcv[NEAR_UP, j, 0] + rcv[NEAR_DOWN, j, 0]
                imag = rcv[NEAR_UP, j, 1] + rcv[NEAR_DOWN, j, 1]
                zero = jnp.zeros_like(real)
                total[2 * j, 0] = total[2 * j, 0] + jnp.where(row < col, real, zero)
                total[2 * j, 1] = total[2 * j, 1] + jnp.where(row < col, imag, jnp.where(row == col, imag * 0.5, zero))
                total[2 * j + 1, 0] = total[2 * j + 1, 0] + jnp.where(row > col, real, zero)
                total[2 * j + 1, 1] = total[2 * j + 1, 1] + jnp.where(row > col, imag, jnp.where(row == col, real * 0.5, zero))
                for n in range(2):
                    write_out(2 * j + n, total)

        each(half + 2, step)

        def close(j):
            for d in range(4):
                ring_copy(d, j).wait_send()

        each(half, close)

    for i in range(4):
        table_copy(i).wait_send()
    each(NE, lambda e: out_copy(e).wait())


def solution(mesh):
    sizes = dict(mesh.shape)

    def on_device(green_lesser, screened, slot_table):
        _, lags, _, rows, cols = green_lesser.shape
        tile = (2, rows, cols)
        half = NE // 2
        f32, dma = jnp.float32, pltpu.SemaphoreType.DMA
        anywhere = pl.BlockSpec(memory_space=pl.ANY)
        return pl.pallas_call(
            functools.partial(kernel, sizes),
            out_shape=jax.ShapeDtypeStruct((1, NE, *tile), f32),
            in_specs=[anywhere, anywhere, pl.BlockSpec(memory_space=pltpu.SMEM)],
            out_specs=anywhere,
            scratch_shapes=[
                pltpu.VMEM((lags, *tile), f32),
                pltpu.VMEM(screened.shape, f32),
                pltpu.SMEM((4, slot_table.shape[0], 1), jnp.int32),
                pltpu.VMEM((4, NE, *tile), f32),
                pltpu.VMEM((4, NE, *tile), f32),
                pltpu.VMEM((4, half, *tile), f32),
                pltpu.VMEM((4, half, *tile), f32),
                pltpu.VMEM((NE, *tile), f32),
                pltpu.VMEM((NE, *tile), f32),
                pltpu.VMEM((NE, *tile), f32),
                pltpu.VMEM((2, *tile), f32),
                dma((2,)),
                dma((4,)),
                dma((4,)),
                dma((4, NE)),
                dma((4, NE)),
                dma((4, half)),
                dma((4, half)),
                dma((NE,)),
                dma((NE,)),
                dma((NE,)),
            ],
            compiler_params=pltpu.CompilerParams(
                collective_id=0, has_side_effects=True, vmem_limit_bytes=48 * 1024 * 1024
            ),
            name="self_energy",
        )(green_lesser, screened, slot_table.reshape(slot_table.shape[0], 1))

    in_specs = (
        P("ka", None, None, "br", "bc"),
        P(None, None, None, "br", "bc"),
        P(None, "ka", None),
    )
    out_specs = P("ka", None, None, "br", "bc")
    return jax.shard_map(on_device, mesh=mesh, in_specs=in_specs, out_specs=out_specs, check_vma=False)
```

```python
import functools

import jax
import jax.numpy as jnp
from jax import lax
from jax.experimental import pallas as pl
from jax.experimental.pallas import tpu as pltpu
from jax.sharding import PartitionSpec as P

NE = 8
NW = 8
GROUP = 2
MESH = pl.DeviceIdType.MESH
FAR_UP, FAR_DOWN, NEAR_UP, NEAR_DOWN = range(4)
HOPS = (2, -2, 1, -1)
STOPS = (3, 4, 1, 2)
STEPS = (1, -1, 1, -1)


def kernel(
    sizes, green_hbm, screened_hbm, table_hbm, out_hbm,
    table, green, screened, tables, src, rcv, give, take, total, mirror, result, work,
    load_sem, table_send, table_recv, ring_send, ring_recv, pair_send, pair_recv,
    mirror_send, mirror_recv, out_sem,
):
    n_ka = sizes["ka"]
    k, r, c = lax.axis_index("ka"), lax.axis_index("br"), lax.axis_index("bc")
    is_diag = r == c
    is_near = (r // GROUP == c // GROUP) & (r != c)
    is_far = r // GROUP != c // GROUP
    partner = (k, c, r)

    def at_hop(hop):
        return (lax.rem(k + hop + n_ka, n_ka), r, c)

    barrier = pltpu.get_barrier_semaphore()
    for hop in HOPS:
        pl.semaphore_signal(barrier, inc=1, device_id=at_hop(hop), device_id_type=MESH)

    @pl.when(jnp.logical_not(is_diag))
    def _():
        pl.semaphore_signal(barrier, inc=1, device_id=partner, device_id_type=MESH)

    loads = [
        pltpu.make_async_copy(green_hbm.at[0], green, load_sem.at[0]),
        pltpu.make_async_copy(screened_hbm, screened, load_sem.at[1]),
        pltpu.make_async_copy(table_hbm, table, load_sem.at[2]),
    ]
    for load in loads:
        load.start()

    @pl.when(is_diag)
    def _():
        pl.semaphore_wait(barrier, len(HOPS))

    @pl.when(jnp.logical_not(is_diag))
    def _():
        pl.semaphore_wait(barrier, len(HOPS) + 1)

    def table_copy(i):
        return pltpu.make_async_remote_copy(
            src_ref=table, dst_ref=tables.at[i], send_sem=table_send.at[i], recv_sem=table_recv.at[i],
            device_id=at_hop(-HOPS[i]), device_id_type=MESH,
        )

    loads[2].wait()
    for i in range(4):
        table_copy(i).start()
    for load in loads[:2]:
        load.wait()
    tile_rows = green.shape[2]

    def terms(dsts, slot, first, added=None, start=0, size=tile_rows):
        count = len(dsts)

        def block(i, carry):
            rows = pl.ds(pl.multiple_of(start + i * 8, 8), 8)
            real, imag = [None] * count, [None] * count
            window = [[green[first + lag, part, rows, :] for part in range(2)] for lag in range(count + NW - 1)]
            for w in range(NW):
                wr, wi = screened[slot, w, 0, rows, :], screened[slot, w, 1, rows, :]
                for n in range(count):
                    gr, gi = window[n + NW - 1 - w]
                    plus, minus = gr * wi + gi * wr, gr * wr - gi * wi
                    real[n] = -plus if w == 0 else real[n] - plus
                    imag[n] = minus if w == 0 else imag[n] + minus
            for n in range(count):
                if added is not None:
                    real[n] = real[n] + added[0, rows, :]
                    imag[n] = imag[n] + added[1, rows, :]
                dsts[n][0, rows, :] = real[n]
                dsts[n][1, rows, :] = imag[n]
            return carry

        lax.fori_loop(0, size // 8, block, 0)

    def each(count, body):
        def step(i, carry):
            body(i)
            return carry

        lax.fori_loop(0, count, step, 0)

    def own_terms(i):
        terms([total.at[2 * i], total.at[2 * i + 1]], table[0, 0, 0], 2 * i)

    each(NE // 2, own_terms)
    for i in range(4):
        table_copy(i).wait_recv()
    slots = [tables[i, 0, 0, STOPS[i]] for i in range(4)]

    def ring_copy(d, j):
        return pltpu.make_async_remote_copy(
            src_ref=src.at[d, j], dst_ref=rcv.at[d, j], send_sem=ring_send.at[d, j], recv_sem=ring_recv.at[d, j],
            device_id=at_hop(STEPS[d]), device_id_type=MESH,
        )

    def pair_copy(d, j):
        return pltpu.make_async_remote_copy(
            src_ref=give.at[d, j], dst_ref=take.at[d, j], send_sem=pair_send.at[d, j], recv_sem=pair_recv.at[d, j],
            device_id=partner, device_id_type=MESH,
        )

    def mirror_copy(e):
        return pltpu.make_async_remote_copy(
            src_ref=total.at[e], dst_ref=mirror.at[e], send_sem=mirror_send.at[e], recv_sem=mirror_recv.at[e],
            device_id=partner, device_id_type=MESH,
        )

    def out_copy(e):
        return pltpu.make_async_copy(result.at[e], out_hbm.at[0, e], out_sem.at[e])

    def write_out(e, other):
        result[e, 0] = (total[e, 0] - other[e, 0].T) * 0.5
        result[e, 1] = (total[e, 1] + other[e, 1].T) * 0.5
        out_copy(e).start()

    @pl.when(is_far)
    def _():
        piece = tile_rows // 2
        pieces = 2 * NE

        def at(u):
            return lax.div(u, 2), pl.multiple_of(lax.rem(u, 2) * piece, piece)

        def ring_piece(d, u):
            e, start = at(u)
            return pltpu.make_async_remote_copy(
                src_ref=src.at[d, e, :, pl.ds(start, piece)], dst_ref=rcv.at[d, e, :, pl.ds(start, piece)],
                send_sem=ring_send.at[d, u], recv_sem=ring_recv.at[d, u],
                device_id=at_hop(STEPS[d]), device_id_type=MESH,
            )

        def mirror_piece(u):
            e, start = at(u)
            return pltpu.make_async_remote_copy(
                src_ref=total.at[e, :, pl.ds(start, piece)], dst_ref=mirror.at[e, :, pl.ds(start, piece)],
                send_sem=mirror_send.at[u], recv_sem=mirror_recv.at[u],
                device_id=partner, device_id_type=MESH,
            )

        def step(i):
            @pl.when(i < pieces)
            def _():
                e, start = at(i)
                for d in (FAR_UP, FAR_DOWN):
                    terms([src.at[d, e]], slots[d], e, None, start, piece)
                    ring_piece(d, i).start()

            @pl.when((i >= 3) & (i < pieces + 3))
            def _():
                u = i - 3
                e, start = at(u)
                for d in (NEAR_UP, NEAR_DOWN):
                    ring_piece(d - 2, u).wait_recv()
                    terms([src.at[d, e]], slots[d], e, rcv.at[d - 2, e], start, piece)
                    ring_piece(d, u).start()

            @pl.when((i >= 6) & (i < pieces + 6))
            def _():
                u = i - 6
                e, start = at(u)
                rows = pl.ds(start, piece)
                for d in (NEAR_UP, NEAR_DOWN):
                    ring_piece(d, u).wait_recv()
                total[e, :, rows] = total[e, :, rows] + (rcv[NEAR_UP, e, :, rows] + rcv[NEAR_DOWN, e, :, rows])
                mirror_piece(u).start()

            @pl.when((i >= 10) & (lax.rem(i, 2) == 0))
            def _():
                e = lax.div(i - 10, 2)
                for n in range(2):
                    mirror_piece(2 * e + n).wait_recv()
                write_out(e, mirror)

        each(pieces + 9, step)

        def close(u):
            for d in range(4):
                ring_piece(d, u).wait_send()
            mirror_piece(u).wait_send()

        each(pieces, close)

    half = NE // 2

    @pl.when(is_near)
    def _():
        mine = jnp.where(r < c, 0, half)
        theirs = half - mine

        def offer(i):
            for d in range(4):
                terms([give.at[d, i]], slots[d], theirs + i)
                pair_copy(d, i).start()

        def joined(d, j, added):
            terms([work.at[0]], slots[d], mine + j, added)
            pair_copy(d, j).wait_recv()
            src[d, j, 0] = work[0, 0] - take[d, j, 0].T
            src[d, j, 1] = work[0, 1] + take[d, j, 1].T
            ring_copy(d, j).start()

        def step(i):
            @pl.when(i < half)
            def _():
                offer(i)

            @pl.when((i >= 1) & (i < half + 1))
            def _():
                for d in (FAR_UP, FAR_DOWN):
                    joined(d, i - 1, None)

            @pl.when((i >= 2) & (i < half + 2))
            def _():
                for d in (NEAR_UP, NEAR_DOWN):
                    ring_copy(d - 2, i - 2).wait_recv()
                    joined(d, i - 2, rcv.at[d - 2, i - 2])

            @pl.when(i == half)
            def _():
                each(half, lambda j: mirror_copy(theirs + j).start())

            @pl.when(i >= 3)
            def _():
                j = i - 3
                e = mine + j
                for d in (NEAR_UP, NEAR_DOWN):
                    ring_copy(d, j).wait_recv()
                total[e] = total[e] + (rcv[NEAR_UP, j] + rcv[NEAR_DOWN, j])

            @pl.when(i == half)
            def _():
                for j in range(2):
                    mirror_copy(mine + j).start()

            @pl.when(i > half)
            def _():
                mirror_copy(mine + i - 3).start()

        each(half + 3, step)

        def finish(j):
            for first in (mine, theirs):
                mirror_copy(first + j).wait_recv()
                write_out(first + j, mirror)

        each(half, finish)

        def close(j):
            for d in range(4):
                ring_copy(d, j).wait_send()
                pair_copy(d, j).wait_send()
            mirror_copy(j).wait_send()
            mirror_copy(half + j).wait_send()

        each(half, close)

    @pl.when(is_diag)
    def _():
        row = lax.broadcasted_iota(jnp.int32, (tile_rows, tile_rows), 0)
        col = lax.broadcasted_iota(jnp.int32, (tile_rows, tile_rows), 1)

        def folded(d, j, added):
            terms([work.at[0], work.at[1]], slots[d], 2 * j)
            real = [work[n, 0] - work[n, 0].T for n in range(2)]
            imag = [work[n, 1] + work[n, 1].T for n in range(2)]
            packed_real = jnp.where(row < col, real[0], jnp.where(row > col, real[1], imag[1]))
            packed_imag = jnp.where(row <= col, imag[0], imag[1])
            if added is not None:
                packed_real, packed_imag = packed_real + added[0], packed_imag + added[1]
            src[d, j, 0] = packed_real
            src[d, j, 1] = packed_imag
            ring_copy(d, j).start()

        def step(i):
            @pl.when(i < half)
            def _():
                for d in (FAR_UP, FAR_DOWN):
                    folded(d, i, None)

            @pl.when((i >= 1) & (i < half + 1))
            def _():
                for d in (NEAR_UP, NEAR_DOWN):
                    ring_copy(d - 2, i - 1).wait_recv()
                    folded(d, i - 1, rcv.at[d - 2, i - 1])

            @pl.when(i >= 2)
            def _():
                j = i - 2
                for d in (NEAR_UP, NEAR_DOWN):
                    ring_copy(d, j).wait_recv()
                real = rcv[NEAR_UP, j, 0] + rcv[NEAR_DOWN, j, 0]
                imag = rcv[NEAR_UP, j, 1] + rcv[NEAR_DOWN, j, 1]
                zero = jnp.zeros_like(real)
                total[2 * j, 0] = total[2 * j, 0] + jnp.where(row < col, real, zero)
                total[2 * j, 1] = total[2 * j, 1] + jnp.where(row < col, imag, jnp.where(row == col, imag * 0.5, zero))
                total[2 * j + 1, 0] = total[2 * j + 1, 0] + jnp.where(row > col, real, zero)
                total[2 * j + 1, 1] = total[2 * j + 1, 1] + jnp.where(row > col, imag, jnp.where(row == col, real * 0.5, zero))
                for n in range(2):
                    write_out(2 * j + n, total)

        each(half + 2, step)

        def close(j):
            for d in range(4):
                ring_copy(d, j).wait_send()

        each(half, close)

    for i in range(4):
        table_copy(i).wait_send()
    each(NE, lambda e: out_copy(e).wait())


def solution(mesh):
    sizes = dict(mesh.shape)

    def on_device(green_lesser, screened, slot_table):
        _, lags, _, rows, cols = green_lesser.shape
        tile = (2, rows, cols)
        half = NE // 2
        f32, dma = jnp.float32, pltpu.SemaphoreType.DMA
        in_hbm = pl.BlockSpec(memory_space=pltpu.HBM)
        return pl.pallas_call(
            functools.partial(kernel, sizes),
            out_shape=jax.ShapeDtypeStruct((1, NE, *tile), f32),
            in_specs=[in_hbm, in_hbm, in_hbm],
            out_specs=in_hbm,
            scratch_shapes=[
                pltpu.SMEM((1, 1, slot_table.shape[0]), jnp.int32),
                pltpu.VMEM((lags, *tile), f32),
                pltpu.VMEM(screened.shape, f32),
                pltpu.SMEM((4, 1, 1, slot_table.shape[0]), jnp.int32),
                pltpu.VMEM((4, NE, *tile), f32),
                pltpu.VMEM((4, NE, *tile), f32),
                pltpu.VMEM((4, half, *tile), f32),
                pltpu.VMEM((4, half, *tile), f32),
                pltpu.VMEM((NE, *tile), f32),
                pltpu.VMEM((NE, *tile), f32),
                pltpu.VMEM((NE, *tile), f32),
                pltpu.VMEM((2, *tile), f32),
                dma((3,)),
                dma((4,)),
                dma((4,)),
                dma((4, 2 * NE)),
                dma((4, 2 * NE)),
                dma((4, half)),
                dma((4, half)),
                dma((2 * NE,)),
                dma((2 * NE,)),
                dma((NE,)),
            ],
            compiler_params=pltpu.CompilerParams(
                collective_id=0, has_side_effects=True, vmem_limit_bytes=66_000_000
            ),
            name="self_energy",
        )(green_lesser, screened, slot_table.transpose(1, 2, 0))

    in_specs = (
        P("ka", None, None, "br", "bc"),
        P(None, None, None, "br", "bc"),
        P(None, "ka", None),
    )
    out_specs = P("ka", None, None, "br", "bc")
    return jax.shard_map(on_device, mesh=mesh, in_specs=in_specs, out_specs=out_specs, check_vma=False)
```

```python
import functools

import jax
import jax.numpy as jnp
from jax import lax
from jax.experimental import pallas as pl
from jax.experimental.pallas import tpu as pltpu
from jax.sharding import PartitionSpec as P

NE = 8
NW = 8
GROUP = 2
RUN = 8
WHOLE = NE - 2
RELAYED = 4
MESH = pl.DeviceIdType.MESH
FAR_UP, FAR_DOWN, NEAR_UP, NEAR_DOWN = range(4)
HOPS = (2, -2, 1, -1)
STOPS = (3, 4, 1, 2)
STEPS = (1, -1, 1, -1)


def kernel(
    sizes, green_hbm, screened_hbm, table_hbm, out_hbm,
    table, green, screened, tables, src, rcv, give, take, total, mirror, result, work,
    load_sem, table_send, table_recv, ring_send, ring_recv, pair_send, pair_recv,
    mirror_send, mirror_recv, relay_send, relay_recv, out_sem,
):
    n_ka = sizes["ka"]
    k, r, c = lax.axis_index("ka"), lax.axis_index("br"), lax.axis_index("bc")
    is_diag = r == c
    is_near = (r // GROUP == c // GROUP) & (r != c)
    is_far = r // GROUP != c // GROUP
    partner = (k, c, r)
    at_run_start = lax.rem(k, RUN) == 0
    at_run_end = lax.rem(k, RUN) == RUN - 1
    at_edge = at_run_start | at_run_end
    far_first = (1 - c // GROUP) * GROUP

    def at_hop(hop):
        return (lax.rem(k + hop + n_ka, n_ka), r, c)

    barrier = pltpu.get_barrier_semaphore()

    def greet(device):
        pl.semaphore_signal(barrier, inc=1, device_id=device, device_id_type=MESH)

    for hop in HOPS:
        greet(at_hop(hop))

    @pl.when(jnp.logical_not(is_diag))
    def _():
        greet(partner)

    @pl.when(is_far & at_edge)
    def _():
        greet((k, c, c))
        greet((k, r, r))

    @pl.when(is_far & at_run_start)
    def _():
        greet((at_hop(-1)[0], c, r))

    @pl.when(is_far & at_run_end)
    def _():
        greet((at_hop(1)[0], c, r))

    @pl.when(is_diag & at_edge)
    def _():
        for q in range(GROUP):
            greet((k, far_first + q, c))
            greet((k, c, far_first + q))

    loads = [
        pltpu.make_async_copy(green_hbm.at[0], green, load_sem.at[0]),
        pltpu.make_async_copy(screened_hbm, screened, load_sem.at[1]),
        pltpu.make_async_copy(table_hbm, table, load_sem.at[2]),
    ]
    for load in loads:
        load.start()

    @pl.when(is_diag & jnp.logical_not(at_edge))
    def _():
        pl.semaphore_wait(barrier, len(HOPS))

    @pl.when(is_diag & at_edge)
    def _():
        pl.semaphore_wait(barrier, len(HOPS) + 2 * GROUP)

    @pl.when(is_near | (is_far & jnp.logical_not(at_edge)))
    def _():
        pl.semaphore_wait(barrier, len(HOPS) + 1)

    @pl.when(is_far & at_edge)
    def _():
        pl.semaphore_wait(barrier, len(HOPS) + 4)

    def table_copy(i):
        return pltpu.make_async_remote_copy(
            src_ref=table, dst_ref=tables.at[i], send_sem=table_send.at[i], recv_sem=table_recv.at[i],
            device_id=at_hop(-HOPS[i]), device_id_type=MESH,
        )

    loads[2].wait()
    for i in range(4):
        table_copy(i).start()
    for load in loads[:2]:
        load.wait()
    tile_rows = green.shape[2]

    def terms(dsts, slot, first, added=None, start=0, size=tile_rows):
        count = len(dsts)

        def block(i, carry):
            rows = pl.ds(pl.multiple_of(start + i * 8, 8), 8)
            real, imag = [None] * count, [None] * count
            window = [[green[first + lag, part, rows, :] for part in range(2)] for lag in range(count + NW - 1)]
            for w in range(NW):
                wr, wi = screened[slot, w, 0, rows, :], screened[slot, w, 1, rows, :]
                for n in range(count):
                    gr, gi = window[n + NW - 1 - w]
                    plus, minus = gr * wi + gi * wr, gr * wr - gi * wi
                    real[n] = -plus if w == 0 else real[n] - plus
                    imag[n] = minus if w == 0 else imag[n] + minus
            for n in range(count):
                if added is not None:
                    real[n] = real[n] + added[0, rows, :]
                    imag[n] = imag[n] + added[1, rows, :]
                dsts[n][0, rows, :] = real[n]
                dsts[n][1, rows, :] = imag[n]
            return carry

        lax.fori_loop(0, size // 8, block, 0)

    def each(count, body):
        def step(i, carry):
            body(i)
            return carry

        lax.fori_loop(0, count, step, 0)

    def own_terms(i):
        terms([total.at[2 * i], total.at[2 * i + 1]], table[0, 0, 0], 2 * i)

    each(NE // 2, own_terms)
    for i in range(4):
        table_copy(i).wait_recv()
    slots = [tables[i, 0, 0, STOPS[i]] for i in range(4)]

    def ring_copy(d, j):
        return pltpu.make_async_remote_copy(
            src_ref=src.at[d, j], dst_ref=rcv.at[d, j], send_sem=ring_send.at[d, j], recv_sem=ring_recv.at[d, j],
            device_id=at_hop(STEPS[d]), device_id_type=MESH,
        )

    def pair_copy(d, j):
        return pltpu.make_async_remote_copy(
            src_ref=give.at[d, j], dst_ref=take.at[d, j], send_sem=pair_send.at[d, j], recv_sem=pair_recv.at[d, j],
            device_id=partner, device_id_type=MESH,
        )

    def mirror_copy(e):
        return pltpu.make_async_remote_copy(
            src_ref=total.at[e], dst_ref=mirror.at[e], send_sem=mirror_send.at[e], recv_sem=mirror_recv.at[e],
            device_id=partner, device_id_type=MESH,
        )

    def out_copy(e):
        return pltpu.make_async_copy(result.at[e], out_hbm.at[0, e], out_sem.at[e])

    def write_out(e, other):
        result[e, 0] = (total[e, 0] - other[e, 0].T) * 0.5
        result[e, 1] = (total[e, 1] + other[e, 1].T) * 0.5
        out_copy(e).start()

    piece = tile_rows // 2

    def at(u):
        return lax.div(u, 2), pl.multiple_of(lax.rem(u, 2) * piece, piece)

    @pl.when(is_far)
    def _():
        slots_used = WHOLE + 1
        pieces = 2 * slots_used
        mine = jnp.where(r < c, WHOLE, WHOLE + 1)
        theirs = 2 * WHOLE + 1 - mine

        def crosses(d, j, sending):
            rising = STEPS[d] > 0
            edge = at_run_end if rising == sending else at_run_start
            return edge & (lax.rem(j, 2) == 1)

        def ring_piece(d, u):
            j, start = at(u)
            turn = crosses(d, j, True).astype(jnp.int32)
            return pltpu.make_async_remote_copy(
                src_ref=src.at[d, j, :, pl.ds(start, piece)], dst_ref=rcv.at[d, j, :, pl.ds(start, piece)],
                send_sem=ring_send.at[d, u], recv_sem=ring_recv.at[d, u],
                device_id=(at_hop(STEPS[d])[0], r + turn * (c - r), c + turn * (r - c)), device_id_type=MESH,
            )

        def arrive(d, u):
            j, _ = at(u)
            turned = crosses(d, j, False)

            @pl.when(jnp.logical_not(turned))
            def _():
                ring_piece(d, u).wait_recv()

            @pl.when(turned & (lax.rem(u, 2) == 0))
            def _():
                for n in range(2):
                    ring_piece(d, u + n).wait_recv()
                rcv[d, j, 0] = -rcv[d, j, 0].T
                rcv[d, j, 1] = rcv[d, j, 1].T

        def mirror_piece(u):
            e, start = at(u)
            return pltpu.make_async_remote_copy(
                src_ref=total.at[e, :, pl.ds(start, piece)], dst_ref=mirror.at[e, :, pl.ds(start, piece)],
                send_sem=mirror_send.at[u], recv_sem=mirror_recv.at[u],
                device_id=partner, device_id_type=MESH,
            )

        def relayed_piece(u):
            e, start = at(u)
            q = lax.rem(r, GROUP)
            return pltpu.make_async_remote_copy(
                src_ref=total.at[e, :, pl.ds(start, piece)],
                dst_ref=take.at[2 * q + lax.div(e, 4), lax.rem(e, 4), :, pl.ds(start, piece)],
                send_sem=mirror_send.at[u], recv_sem=relay_recv.at[q, u],
                device_id=(k, c, c), device_id_type=MESH,
            )

        def send_mirror(u):
            relayed = at_edge & (u < 2 * RELAYED)

            @pl.when(relayed)
            def _():
                relayed_piece(u).start()

            @pl.when(jnp.logical_not(relayed))
            def _():
                mirror_piece(u).start()

        def offer(d):
            terms([give.at[d, 0]], slots[d], theirs)
            pair_copy(d, 0).start()

        def joined(d, added):
            terms([work.at[0]], slots[d], mine, added)
            pair_copy(d, 0).wait_recv()
            src[d, WHOLE, 0] = work[0, 0] - take[d, 0, 0].T
            src[d, WHOLE, 1] = work[0, 1] + take[d, 0, 1].T
            for n in range(2):
                ring_piece(d, 2 * WHOLE + n).start()

        def step(i):
            @pl.when(i < 2 * WHOLE)
            def _():
                j, start = at(i)
                for d in (FAR_UP, FAR_DOWN):
                    terms([src.at[d, j]], slots[d], j, None, start, piece)
                    ring_piece(d, i).start()

            for d in range(4):
                @pl.when(i == d + 1)
                def _():
                    offer(d)

            @pl.when(i == 2 * WHOLE)
            def _():
                for d in (FAR_UP, FAR_DOWN):
                    joined(d, None)

            @pl.when((i >= 5) & (i < 2 * WHOLE + 5))
            def _():
                u = i - 5
                j, start = at(u)
                for d in (NEAR_UP, NEAR_DOWN):
                    arrive(d - 2, u)
                    terms([src.at[d, j]], slots[d], j, rcv.at[d - 2, j], start, piece)
                    ring_piece(d, u).start()

            @pl.when(i == 2 * WHOLE + 5)
            def _():
                for d in (NEAR_UP, NEAR_DOWN):
                    for n in range(2):
                        ring_piece(d - 2, 2 * WHOLE + n).wait_recv()
                    joined(d, rcv.at[d - 2, WHOLE])

            @pl.when(i == 6)
            def _():
                for n in range(2):
                    mirror_piece(2 * theirs + n).start()

            @pl.when((i >= 10) & (i < pieces + 10))
            def _():
                u = i - 10
                j, start = at(u)
                e = jnp.where(j == WHOLE, mine, j)
                rows = pl.ds(start, piece)
                for d in (NEAR_UP, NEAR_DOWN):
                    arrive(d, u)
                total[e, :, rows] = total[e, :, rows] + (rcv[NEAR_UP, j, :, rows] + rcv[NEAR_DOWN, j, :, rows])
                send_mirror(2 * e + lax.rem(u, 2))

            @pl.when((i >= 20) & (i < 20 + 2 * WHOLE) & (lax.rem(i - 20, 2) == 0))
            def _():
                e = lax.div(i - 20, 2)
                for n in range(2):
                    mirror_piece(2 * e + n).wait_recv()
                write_out(e, mirror)

        each(max(20 + 2 * WHOLE - 1, pieces + 10), step)
        for e in (mine, theirs):
            for n in range(2):
                mirror_piece(2 * e + n).wait_recv()
            write_out(e, mirror)

        def close(u):
            for d in range(4):
                ring_piece(d, u).wait_send()

        each(pieces, close)
        each(2 * NE, lambda u: mirror_piece(u).wait_send())
        for d in range(4):
            pair_copy(d, 0).wait_send()

    half = NE // 2

    @pl.when(is_near)
    def _():
        mine = jnp.where(r < c, 0, half)
        theirs = half - mine

        def offer(i):
            for d in range(4):
                terms([give.at[d, i]], slots[d], theirs + i)
                pair_copy(d, i).start()

        def joined(d, j, added):
            terms([work.at[0]], slots[d], mine + j, added)
            pair_copy(d, j).wait_recv()
            src[d, j, 0] = work[0, 0] - take[d, j, 0].T
            src[d, j, 1] = work[0, 1] + take[d, j, 1].T
            ring_copy(d, j).start()

        def step(i):
            @pl.when(i < half)
            def _():
                offer(i)

            @pl.when((i >= 1) & (i < half + 1))
            def _():
                for d in (FAR_UP, FAR_DOWN):
                    joined(d, i - 1, None)

            @pl.when((i >= 2) & (i < half + 2))
            def _():
                for d in (NEAR_UP, NEAR_DOWN):
                    ring_copy(d - 2, i - 2).wait_recv()
                    joined(d, i - 2, rcv.at[d - 2, i - 2])

            @pl.when(i == half)
            def _():
                each(half, lambda j: mirror_copy(theirs + j).start())

            @pl.when(i >= 3)
            def _():
                j = i - 3
                e = mine + j
                for d in (NEAR_UP, NEAR_DOWN):
                    ring_copy(d, j).wait_recv()
                total[e] = total[e] + (rcv[NEAR_UP, j] + rcv[NEAR_DOWN, j])

            @pl.when(i == half)
            def _():
                for j in range(2):
                    mirror_copy(mine + j).start()

            @pl.when(i > half)
            def _():
                mirror_copy(mine + i - 3).start()

        each(half + 3, step)

        def finish(j):
            for first in (mine, theirs):
                mirror_copy(first + j).wait_recv()
                write_out(first + j, mirror)

        each(half, finish)

        def close(j):
            for d in range(4):
                ring_copy(d, j).wait_send()
                pair_copy(d, j).wait_send()
            mirror_copy(j).wait_send()
            mirror_copy(half + j).wait_send()

        each(half, close)

    @pl.when(is_diag)
    def _():
        row = lax.broadcasted_iota(jnp.int32, (tile_rows, tile_rows), 0)
        col = lax.broadcasted_iota(jnp.int32, (tile_rows, tile_rows), 1)

        def folded(d, j, added):
            terms([work.at[0], work.at[1]], slots[d], 2 * j)
            real = [work[n, 0] - work[n, 0].T for n in range(2)]
            imag = [work[n, 1] + work[n, 1].T for n in range(2)]
            packed_real = jnp.where(row < col, real[0], jnp.where(row > col, real[1], imag[1]))
            packed_imag = jnp.where(row <= col, imag[0], imag[1])
            if added is not None:
                packed_real, packed_imag = packed_real + added[0], packed_imag + added[1]
            src[d, j, 0] = packed_real
            src[d, j, 1] = packed_imag
            ring_copy(d, j).start()

        def step(i):
            @pl.when(i < half)
            def _():
                for d in (FAR_UP, FAR_DOWN):
                    folded(d, i, None)

            @pl.when((i >= 1) & (i < half + 1))
            def _():
                for d in (NEAR_UP, NEAR_DOWN):
                    ring_copy(d - 2, i - 1).wait_recv()
                    folded(d, i - 1, rcv.at[d - 2, i - 1])

        def finish(j):
            for d in (NEAR_UP, NEAR_DOWN):
                ring_copy(d, j).wait_recv()
            real = rcv[NEAR_UP, j, 0] + rcv[NEAR_DOWN, j, 0]
            imag = rcv[NEAR_UP, j, 1] + rcv[NEAR_DOWN, j, 1]
            zero = jnp.zeros_like(real)
            total[2 * j, 0] = total[2 * j, 0] + jnp.where(row < col, real, zero)
            total[2 * j, 1] = total[2 * j, 1] + jnp.where(row < col, imag, jnp.where(row == col, imag * 0.5, zero))
            total[2 * j + 1, 0] = total[2 * j + 1, 0] + jnp.where(row > col, real, zero)
            total[2 * j + 1, 1] = total[2 * j + 1, 1] + jnp.where(row > col, imag, jnp.where(row == col, real * 0.5, zero))
            for n in range(2):
                write_out(2 * j + n, total)

        each(half + 1, step)

        def passed_on(q, u):
            e, start = at(u)
            return pltpu.make_async_remote_copy(
                src_ref=take.at[2 * q + lax.div(e, 4), lax.rem(e, 4), :, pl.ds(start, piece)],
                dst_ref=mirror.at[e, :, pl.ds(start, piece)],
                send_sem=relay_send.at[q, u], recv_sem=mirror_recv.at[u],
                device_id=(k, c, far_first + q), device_id_type=MESH,
            )

        def came_in(q, u):
            e, start = at(u)
            held = take.at[2 * q + lax.div(e, 4), lax.rem(e, 4), :, pl.ds(start, piece)]
            return pltpu.make_async_remote_copy(
                src_ref=total.at[e, :, pl.ds(start, piece)], dst_ref=held,
                send_sem=relay_send.at[q, u], recv_sem=relay_recv.at[q, u],
                device_id=(k, far_first + q, c), device_id_type=MESH,
            )

        @pl.when(at_edge)
        def _():
            def relay(u):
                for q in range(GROUP):
                    came_in(q, u).wait_recv()
                    passed_on(q, u).start()

            each(2 * RELAYED, relay)

        each(half, finish)

        @pl.when(at_edge)
        def _():
            def relayed(u):
                for q in range(GROUP):
                    passed_on(q, u).wait_send()

            each(2 * RELAYED, relayed)

        def close(j):
            for d in range(4):
                ring_copy(d, j).wait_send()

        each(half, close)

    for i in range(4):
        table_copy(i).wait_send()
    each(NE, lambda e: out_copy(e).wait())


def solution(mesh):
    sizes = dict(mesh.shape)

    def on_device(green_lesser, screened, slot_table):
        _, lags, _, rows, cols = green_lesser.shape
        tile = (2, rows, cols)
        half = NE // 2
        f32, dma = jnp.float32, pltpu.SemaphoreType.DMA
        in_hbm = pl.BlockSpec(memory_space=pltpu.HBM)
        return pl.pallas_call(
            functools.partial(kernel, sizes),
            out_shape=jax.ShapeDtypeStruct((1, NE, *tile), f32),
            in_specs=[in_hbm, in_hbm, in_hbm],
            out_specs=in_hbm,
            scratch_shapes=[
                pltpu.SMEM((1, 1, slot_table.shape[0]), jnp.int32),
                pltpu.VMEM((lags, *tile), f32),
                pltpu.VMEM(screened.shape, f32),
                pltpu.SMEM((4, 1, 1, slot_table.shape[0]), jnp.int32),
                pltpu.VMEM((4, NE, *tile), f32),
                pltpu.VMEM((4, NE, *tile), f32),
                pltpu.VMEM((4, half, *tile), f32),
                pltpu.VMEM((4, half, *tile), f32),
                pltpu.VMEM((NE, *tile), f32),
                pltpu.VMEM((NE, *tile), f32),
                pltpu.VMEM((NE, *tile), f32),
                pltpu.VMEM((2, *tile), f32),
                dma((3,)),
                dma((4,)),
                dma((4,)),
                dma((4, 2 * NE)),
                dma((4, 2 * NE)),
                dma((4, half)),
                dma((4, half)),
                dma((2 * NE,)),
                dma((2 * NE,)),
                dma((2, 2 * NE)),
                dma((2, 2 * NE)),
                dma((NE,)),
            ],
            compiler_params=pltpu.CompilerParams(
                collective_id=0, has_side_effects=True, vmem_limit_bytes=66_000_000
            ),
            name="self_energy",
        )(green_lesser, screened, slot_table.transpose(1, 2, 0))

    in_specs = (
        P("ka", None, None, "br", "bc"),
        P(None, None, None, "br", "bc"),
        P(None, "ka", None),
    )
    out_specs = P("ka", None, None, "br", "bc")
    return jax.shard_map(on_device, mesh=mesh, in_specs=in_specs, out_specs=out_specs, check_vma=False)
```
